768 devices in a mesh: grp: 96 (over z, y), blk: 8 (over x, core).
Axes of the slice: x: 4, y: 8, z: 12, core: 2. Of those that a mesh axis runs over, the one named last changes fastest.
Arguments:
- source: bfloat16 [786432, 256], P(('grp', 'blk')), may hold values from -6 to 6
- send_ids: int32 [768, 16], P(('grp', 'blk')), may hold values from 0 to 15
- send_counts: int32 [768, 8], P(('grp', 'blk')), may hold values from 1 to 2, as said below
- tile_slot: int32 [768, 128], P(('grp', 'blk')), may hold values from 0 to 15, as said below
- tile_target: int32 [768, 128], P(('grp', 'blk')), may hold values from 0 to 63, as said below
- tile_weights: bfloat16 [98304, 4096], P(('grp', 'blk')), may hold values from 0 to 0.0625
Outputs:
- remapped: float32 [1572864, 256], P(('grp', 'blk'))
The draws below stay inside these ranges and needn't reach their ends.
Inputs may be any that keep to these rules, and one draw needn't show every extreme that they name: `send_counts`: every reader of every partition is sent at least one block, and each partition sends 2 blocks to some reader. `tile_slot`: each of the 8 * 2 receive slots is read by at least one tile of every partition. `tile_target`: each of the 64 partial target blocks is written by at least one tile of every partition.
All inputs are finite; a program needn't handle non-finite values.
Results may differ from the reference program's by a relative error of at most 0.0003.
Values may be sent and summed in bfloat16 or wider, within the bound.
A program may use at most 32 MiB of HBM per device.

```python
from functools import partial
import jax
import jax.numpy as jnp
from jax import lax

COLS = 256
BLOCK = 64
SB = 16
CAP = 2
TB = 32
EB = 16
NT = 128
PARTITIONS = 768
N_BLK = 8


def tile_lists(key):
    base_key = jax.random.fold_in(key, 17)
    target_key, slot_key, order_key = jax.random.split(base_key, 3)
    segments = TB + 2 * EB
    slot_total = N_BLK * CAP
    extra_targets = jax.random.randint(target_key, (PARTITIONS, NT - segments), 0, segments, dtype=jnp.int32)
    targets = jnp.concatenate([jnp.broadcast_to(jnp.arange(segments, dtype=jnp.int32)[None, :], (PARTITIONS, segments)), extra_targets], axis=1)
    extra_slots = jax.random.randint(slot_key, (PARTITIONS, NT - slot_total), 0, slot_total, dtype=jnp.int32)
    slots_all = jnp.concatenate([jnp.broadcast_to(jnp.arange(slot_total, dtype=jnp.int32)[None, :], (PARTITIONS, slot_total)), extra_slots], axis=1)
    row_keys = jax.random.split(order_key, PARTITIONS)
    orders = jax.vmap(lambda row_key: jax.random.permutation(row_key, NT))(row_keys).astype(jnp.int32)
    return (jnp.take_along_axis(targets, orders, axis=1), jnp.take_along_axis(slots_all, orders, axis=1))


def draw_tile_slot(key, part):
    return tile_lists(key)[1]


def draw_tile_target(key, part):
    return tile_lists(key)[0]


def draw_send_counts(key, part):
    count_key, peak_key = jax.random.split(jax.random.fold_in(key, 5))
    counts = jax.random.randint(count_key, (PARTITIONS, N_BLK), 1, CAP + 1, dtype=jnp.int32)
    peak_reader = jax.random.randint(peak_key, (PARTITIONS, 1), 0, N_BLK, dtype=jnp.int32)
    readers = jnp.arange(N_BLK, dtype=jnp.int32)[None, :]
    return jnp.where(readers == peak_reader, CAP, counts).astype(jnp.int32)


def plant(drawn, key, low, largest):
    shape = drawn.shape
    spot = [jax.random.randint(jax.random.fold_in(key, axis), (), 0, shape[axis]) for axis in range(len(shape))]
    drawn = drawn.at[tuple(spot)].set(low)
    longest = shape.index(max(shape))
    spot[longest] = (spot[longest] + 1) % shape[longest]
    return drawn.at[tuple(spot)].set(largest)


def level_of(stream_key, extent, cuts, low, high):
    gain = 1.0
    for dim, parts in cuts:
        heights = jax.random.uniform(jax.random.fold_in(jax.random.fold_in(stream_key, 6), dim), (parts,), jnp.float32, low / len(cuts), high / len(cuts))
        gain = gain * jnp.repeat(jnp.exp(heights), extent[dim] // parts).reshape((-1,) + (1,) * (len(extent) - 1 - dim))
    return gain


def noise(stream_key, extent, spread, most, shards=(), kind=jnp.bfloat16):
    result = jax.random.normal(stream_key, extent, jnp.float32) * spread
    if len(shards) > 0:
        result = level_of(stream_key, extent, shards, -0.22, 0.18) * result
    return jnp.clip(result, min=-most, max=most).astype(kind)


def setup_inputs(seed: int = 0) -> dict:
    key_of = jax.random.split(jax.random.key(seed), 7)
    source = noise(key_of[0], (PARTITIONS * SB * BLOCK, COLS), 1.0, 6.0, ((0, 768),))
    send_ids = plant(jax.random.randint(key_of[1], (PARTITIONS, N_BLK * CAP), 0, SB), jax.random.fold_in(key_of[1], 1), 0, SB - 1).astype(jnp.int32)
    send_counts = draw_send_counts(jax.random.fold_in(key_of[6], 71), 0)
    tile_slot = draw_tile_slot(jax.random.fold_in(key_of[6], 71), 0)
    tile_target = draw_tile_target(jax.random.fold_in(key_of[6], 71), 0)
    tile_weights = jnp.clip(0.0625 * jax.random.uniform(key_of[5], (PARTITIONS * NT, BLOCK * BLOCK), jnp.float32) ** level_of(key_of[5], (PARTITIONS * NT, BLOCK * BLOCK), ((0, 768),), -0.2, 0.2), 0.0, 0.0625).astype(jnp.bfloat16)
    return dict(source=source, send_ids=send_ids, send_counts=send_counts, tile_slot=tile_slot, tile_target=tile_target, tile_weights=tile_weights)


def device_partial(device, source, send_ids, send_counts, tile_slot, tile_target, tile_weights):
    group_index = device // N_BLK
    reader_index = device % N_BLK
    senders = group_index * N_BLK + jnp.arange(N_BLK, dtype=jnp.int32)
    sender_ids = jnp.take(send_ids, senders, axis=0)
    block_ids = lax.dynamic_slice_in_dim(sender_ids, reader_index * CAP, CAP, 1)
    sender_counts = jnp.take(send_counts, senders, axis=0)
    live_counts = lax.dynamic_slice_in_dim(sender_counts, reader_index, 1, 1)[:, 0]
    source_blocks = source.reshape(PARTITIONS, SB, BLOCK, COLS)
    chosen = source_blocks[senders[:, None], block_ids]
    live_mask = jnp.arange(CAP, dtype=jnp.int32)[None, :] < live_counts[:, None]
    chosen = jnp.where(live_mask[:, :, None, None], chosen, jnp.zeros_like(chosen))
    received = chosen.reshape(N_BLK * CAP, BLOCK, COLS)
    tile_slots = lax.dynamic_index_in_dim(tile_slot, device, 0, keepdims=False)
    tile_targets = lax.dynamic_index_in_dim(tile_target, device, 0, keepdims=False)
    operands = jnp.take(received, tile_slots, axis=0).astype(jnp.float32)
    weights = lax.dynamic_slice_in_dim(tile_weights, device * NT, NT, 0)
    weights = weights.reshape(NT, BLOCK, BLOCK).astype(jnp.float32)
    products = jnp.einsum("kij,kjc->kic", weights, operands, precision=lax.Precision.HIGHEST)
    return jax.ops.segment_sum(products, tile_targets, num_segments=TB + 2 * EB)


def reference(source, send_ids, send_counts, tile_slot, tile_target, tile_weights):
    compute = partial(device_partial, source=source, send_ids=send_ids, send_counts=send_counts,
                      tile_slot=tile_slot, tile_target=tile_target, tile_weights=tile_weights)
    first_pieces = compute(jnp.int32(0))
    final_pieces = compute(jnp.int32(PARTITIONS - 1))

    def advance(running, device):
        prior_own, prior_upper = running
        pieces = compute(device)
        lower_edge = pieces[:EB]
        middle = pieces[EB:EB + TB]
        upper_edge = pieces[EB + TB:]
        finished = jnp.concatenate([prior_own[:TB - EB], prior_own[TB - EB:] + lower_edge], axis=0)
        current = jnp.concatenate([middle[:EB] + prior_upper, middle[EB:]], axis=0)
        return (current, upper_edge), finished

    start_running = (jnp.zeros((TB, BLOCK, COLS), jnp.float32), final_pieces[EB + TB:])
    devices = jnp.arange(PARTITIONS, dtype=jnp.int32)
    (last_own, last_upper), emitted = lax.scan(advance, start_running, devices)
    last_done = jnp.concatenate([last_own[:TB - EB], last_own[TB - EB:] + first_pieces[:EB]], axis=0)
    assembled = jnp.concatenate([emitted[1:], last_done[None]], axis=0)
    return assembled.reshape(PARTITIONS * TB * BLOCK, COLS)
```

```python
import functools

import jax
import jax.numpy as jnp
from jax import lax
from jax.experimental import pallas as pl
from jax.experimental.pallas import tpu as pltpu
from jax.sharding import PartitionSpec as P

COLS = 256
BLOCK = 64
TB = 32
EB = 16
SEG = TB + 2 * EB
CHUNKS = 1
UNROLL = 8
ORDER = (4, 3, 5, 2, 6, 1, 7)
STEPS = 32766.0
MESH = pl.DeviceIdType.MESH


def tables(slot_ref, target_ref, table_ref):
    count = slot_ref.shape[1]
    key = (target_ref[...] + EB) % SEG
    across = jnp.broadcast_to(key, (count, count))
    down = across.T
    row = lax.broadcasted_iota(jnp.int32, (count, count), 0)
    col = lax.broadcasted_iota(jnp.int32, (count, count), 1)
    ahead = (down < across) | ((down == across) & (row < col))
    rank = jnp.sum(ahead.astype(jnp.int32), axis=0, keepdims=True)
    packed = lax.broadcasted_iota(jnp.int32, (1, count), 1) + 128 * slot_ref[...] + 2048 * key
    rank_down = jnp.broadcast_to(rank, (count, count)).T
    packed_down = jnp.broadcast_to(packed, (count, count)).T
    ordered = jnp.sum(jnp.where(rank_down == col, packed_down, 0), axis=0, keepdims=True)
    goal = ordered >> 11
    same = (goal == pltpu.roll(goal, 1, 1)) & (lax.broadcasted_iota(jnp.int32, (1, count), 1) > 0)
    table_ref[0:1, :] = ordered & 127
    table_ref[1:2, :] = (ordered >> 7) & 15
    table_ref[2:3, :] = same.astype(jnp.int32)
    upto = jnp.sum((down <= col).astype(jnp.int32), axis=0, keepdims=True)
    table_ref[3:4, :] = jnp.maximum(upto - 1, 0)


def kernel(
    groups, size,
    ids_ref, counts_ref, slot_ref, target_ref, source_hbm, weights_hbm, out_ref,
    source, flat, tiles, outgoing, received, sums, table, table_s,
    edge_out, scale_out, edge_in, scale_in,
    local_sem, send_sem, recv_sem, edge_send, edge_recv,
):
    group, me = lax.axis_index("grp"), lax.axis_index("blk")
    count = slot_ref.shape[1]
    width = COLS // CHUNKS
    cap = ids_ref.shape[1] // size
    after = ((group + (me + 1) // size) % groups, (me + 1) % size)
    before = ((group + groups - 1 + (me + size - 1) // size) % groups, (me + size - 1) % size)

    barrier = pltpu.get_barrier_semaphore()
    for k in range(1, size):
        pl.semaphore_signal(barrier, inc=1, device_id=(group, (me + k) % size), device_id_type=MESH)
    pl.semaphore_signal(barrier, inc=1, device_id=after, device_id_type=MESH)
    pl.semaphore_signal(barrier, inc=1, device_id=before, device_id_type=MESH)

    load_source = pltpu.make_async_copy(source_hbm, source, local_sem.at[0])
    load_weights = pltpu.make_async_copy(weights_hbm, flat, local_sem.at[1])
    load_source.start()
    load_weights.start()
    load_source.wait()

    sends = []
    for c in range(CHUNKS):
        columns = slice(c * width, (c + 1) * width)
        for k in (0,) + ORDER:
            reader = (me + k) % size
            live = counts_ref[0, reader]
            for j in range(cap):
                block = source[ids_ref[0, reader * cap + j], :, columns]
                kept = jnp.clip(live - j, 0, 1).astype(jnp.float32)
                block = block * jnp.full(block.shape, kept, jnp.float32).astype(block.dtype)
                if k == 0:
                    received[c, me * cap + j] = block
                else:
                    outgoing[c, k, j] = block
    pl.semaphore_wait(barrier, size + 1)
    for c in range(CHUNKS):
        sends.append({})
        for k in ORDER:
            copy = pltpu.make_async_remote_copy(
                src_ref=outgoing.at[c, k],
                dst_ref=received.at[c, pl.ds(me * cap, cap)],
                send_sem=send_sem.at[c, k],
                recv_sem=recv_sem.at[c, k],
                device_id=(group, (me + k) % size),
                device_id_type=MESH,
            )
            copy.start()
            sends[c][k] = copy

    tables(slot_ref, target_ref, table)
    fill = pltpu.make_async_copy(table, table_s, local_sem.at[2])
    fill.start()
    load_weights.wait()

    rows = tiles.reshape(count * BLOCK, 2 * BLOCK)

    @pl.loop(0, count // 16)
    def _(a):
        first = pl.multiple_of(a * 16, 16)
        for i in range(0, BLOCK, 2):
            pair = flat[pl.ds(first, 16), i * BLOCK : (i + 2) * BLOCK].astype(jnp.float32)
            rows[pl.ds(first * BLOCK + i, 16, stride=BLOCK), :] = pair
            rows[pl.ds(first * BLOCK + i + 1, 16, stride=BLOCK), :] = pltpu.roll(pair, BLOCK, 1)

    fill.wait()

    def send_edge(c, side):
        dest = after if side == 0 else before
        copies = []
        for n, (src, dst) in enumerate(((edge_out, edge_in), (scale_out, scale_in))):
            copy = pltpu.make_async_remote_copy(
                src_ref=src.at[c, side],
                dst_ref=dst.at[c, side],
                send_sem=edge_send.at[c, side, n],
                recv_sem=edge_recv.at[c, side, n],
                device_id=dest,
                device_id_type=MESH,
            )
            copy.start()
            copies.append(copy)
        return copies

    edges = []
    for c in range(CHUNKS):
        columns = slice(c * width, (c + 1) * width)
        for k in ORDER:
            sends[c][k].wait_recv()

        def run(step, total):
            for u in range(UNROLL):
                place = step * UNROLL + u
                block = received[c, table_s[1, place]]
                tile = tiles[table_s[0, place]][:, :BLOCK].astype(jnp.bfloat16)
                part = jnp.dot(tile, block, preferred_element_type=jnp.float32)
                total = part + total * table_s[2, place].astype(jnp.float32)
                sums[place] = total
            return total

        lax.fori_loop(0, count // UNROLL, run, jnp.zeros((BLOCK, width), jnp.float32))

        edges.append([])
        for side in range(2):

            @pl.loop(0, EB)
            def _(i):
                whole = sums[table_s[3, side * EB + i]]
                most = jnp.maximum(jnp.max(jnp.abs(whole), axis=0, keepdims=True), 1e-30)
                coded = jnp.round(whole * (STEPS / most))
                edge_out[c, side, i] = coded.astype(jnp.int32).astype(jnp.int16)
                scale_out[c, side, i] = most * (1.0 / STEPS)

            edges[c].append(send_edge(c, side))

        @pl.loop(0, TB)
        def _(i):
            out_ref[i, :, columns] = sums[table_s[3, 2 * EB + i]]

    for c in range(CHUNKS):
        columns = slice(c * width, (c + 1) * width)
        for side in range(2):
            for copy in edges[c][side]:
                copy.wait_recv()

            @pl.loop(0, EB)
            def _(i):
                part = edge_in[c, side, i].astype(jnp.int32).astype(jnp.float32) * scale_in[c, side, i]
                spot = i + (0 if side == 0 else TB - EB)
                out_ref[spot, :, columns] = out_ref[spot, :, columns] + part

    for c in range(CHUNKS):
        for k in ORDER:
            sends[c][k].wait_send()
        for side in range(2):
            for copy in edges[c][side]:
                copy.wait_send()


def body(groups, size, source, send_ids, send_counts, tile_slot, tile_target, tile_weights):
    count = tile_weights.shape[0]
    cap = send_ids.shape[1] // size
    width = COLS // CHUNKS
    blocks = source.shape[0] // BLOCK
    smem = pl.BlockSpec(memory_space=pltpu.SMEM)
    vmem = pl.BlockSpec(memory_space=pltpu.VMEM)
    hbm = pl.BlockSpec(memory_space=pl.ANY)
    dma = pltpu.SemaphoreType.DMA
    out = pl.pallas_call(
        functools.partial(kernel, groups, size),
        out_shape=jax.ShapeDtypeStruct((TB, BLOCK, COLS), jnp.float32),
        in_specs=[smem, smem, vmem, vmem, hbm, hbm],
        out_specs=vmem,
        scratch_shapes=[
            pltpu.VMEM((blocks, BLOCK, COLS), jnp.bfloat16),
            pltpu.VMEM((count, BLOCK * BLOCK), jnp.bfloat16),
            pltpu.VMEM((count, BLOCK, 2 * BLOCK), jnp.float32),
            pltpu.VMEM((CHUNKS, size, cap, BLOCK, width), jnp.bfloat16),
            pltpu.VMEM((CHUNKS, size * cap, BLOCK, width), jnp.bfloat16),
            pltpu.VMEM((count, BLOCK, width), jnp.float32),
            pltpu.VMEM((8, count), jnp.int32),
            pltpu.SMEM((8, count), jnp.int32),
            pltpu.VMEM((CHUNKS, 2, EB, BLOCK, width), jnp.int16),
            pltpu.VMEM((CHUNKS, 2, EB, 1, width), jnp.float32),
            pltpu.VMEM((CHUNKS, 2, EB, BLOCK, width), jnp.int16),
            pltpu.VMEM((CHUNKS, 2, EB, 1, width), jnp.float32),
            dma((3,)),
            dma((CHUNKS, size)),
            dma((CHUNKS, size)),
            dma((CHUNKS, 2, 2)),
            dma((CHUNKS, 2, 2)),
        ],
        compiler_params=pltpu.CompilerParams(
            collective_id=0, has_side_effects=True, vmem_limit_bytes=48 << 20
        ),
    )(send_ids, send_counts, tile_slot, tile_target, source.reshape(blocks, BLOCK, COLS), tile_weights)
    return out.reshape(TB * BLOCK, COLS)


def solution(mesh):
    sizes = (mesh.shape["grp"], mesh.shape["blk"])
    return jax.shard_map(
        functools.partial(body, *sizes),
        mesh=mesh,
        in_specs=(P(("grp", "blk"), None),) * 6,
        out_specs=P(("grp", "blk"), None),
        check_vma=False,
    )
```

```python
import functools

import jax
import jax.numpy as jnp
from jax import lax
from jax.experimental import pallas as pl
from jax.experimental.pallas import tpu as pltpu
from jax.sharding import PartitionSpec as P

COLS = 256
BLOCK = 64
TB = 32
EB = 16
SEG = TB + 2 * EB
CHUNKS = 1
UNROLL = 32
ORDER = (4, 3, 5, 2, 6, 1, 7)
STEPS = 32766.0
PIECE = 4
PIECES = [(piece, side) for piece in range(EB // PIECE) for side in range(2)]
MESH = pl.DeviceIdType.MESH


def tables(slot_ref, target_ref, table_ref):
    count = slot_ref.shape[1]
    key = (target_ref[...] + EB) % SEG
    across = jnp.broadcast_to(key, (count, count))
    down = across.T
    row = lax.broadcasted_iota(jnp.int32, (count, count), 0)
    col = lax.broadcasted_iota(jnp.int32, (count, count), 1)
    ahead = (down < across) | ((down == across) & (row < col))
    rank = jnp.sum(ahead.astype(jnp.int32), axis=0, keepdims=True)
    packed = lax.broadcasted_iota(jnp.int32, (1, count), 1) + 128 * slot_ref[...] + 2048 * key
    rank_down = jnp.broadcast_to(rank, (count, count)).T
    packed_down = jnp.broadcast_to(packed, (count, count)).T
    ordered = jnp.sum(jnp.where(rank_down == col, packed_down, 0), axis=0, keepdims=True)
    goal = ordered >> 11
    same = (goal == pltpu.roll(goal, 1, 1)) & (lax.broadcasted_iota(jnp.int32, (1, count), 1) > 0)
    table_ref[0:1, :] = ordered & 127
    table_ref[1:2, :] = (ordered >> 7) & 15
    table_ref[2:3, :] = same.astype(jnp.int32)
    upto = jnp.sum((down <= col).astype(jnp.int32), axis=0, keepdims=True)
    table_ref[3:4, :] = jnp.maximum(upto - 1, 0)


def kernel(
    groups, size,
    ids_hbm, counts_hbm, slot_hbm, target_hbm, source_hbm, weights_hbm, out_ref,
    ids_ref, counts_ref, slot_ref, target_ref, source, flat, tiles, outgoing, received, sums, table, table_s,
    edge_out, scale_out, edge_in, scale_in,
    local_sem, send_sem, recv_sem, edge_send, edge_recv,
):
    group, me = lax.axis_index("grp"), lax.axis_index("blk")
    count = slot_hbm.shape[1]
    width = COLS // CHUNKS
    cap = ids_hbm.shape[1] // size
    after = ((group + (me + 1) // size) % groups, (me + 1) % size)
    before = ((group + groups - 1 + (me + size - 1) // size) % groups, (me + size - 1) % size)

    barrier = pltpu.get_barrier_semaphore()
    for k in range(1, size):
        pl.semaphore_signal(barrier, inc=1, device_id=(group, (me + k) % size), device_id_type=MESH)
    pl.semaphore_signal(barrier, inc=1, device_id=after, device_id_type=MESH)
    pl.semaphore_signal(barrier, inc=1, device_id=before, device_id_type=MESH)

    pairs = (
        (ids_hbm, ids_ref), (counts_hbm, counts_ref), (source_hbm, source),
        (slot_hbm, slot_ref), (target_hbm, target_ref), (weights_hbm, flat),
    )
    loads = [pltpu.make_async_copy(src, dst, local_sem.at[n]) for n, (src, dst) in enumerate(pairs)]
    for load in loads:
        load.start()
    for load in loads[:3]:
        load.wait()

    sends = []
    for c in range(CHUNKS):
        columns = slice(c * width, (c + 1) * width)
        for k in (0,) + ORDER:
            reader = (me + k) % size
            live = counts_ref[0, reader]
            for j in range(cap):
                block = source[ids_ref[0, reader * cap + j], :, columns]
                kept = jnp.clip(live - j, 0, 1).astype(jnp.float32)
                block = block * jnp.full(block.shape, kept, jnp.float32).astype(block.dtype)
                if k == 0:
                    received[c, me * cap + j] = block
                else:
                    outgoing[c, k, j] = block
    pl.semaphore_wait(barrier, size + 1)
    for c in range(CHUNKS):
        sends.append({})
        for k in ORDER:
            copy = pltpu.make_async_remote_copy(
                src_ref=outgoing.at[c, k],
                dst_ref=received.at[c, pl.ds(me * cap, cap)],
                send_sem=send_sem.at[c, k],
                recv_sem=recv_sem.at[c, k],
                device_id=(group, (me + k) % size),
                device_id_type=MESH,
            )
            copy.start()
            sends[c][k] = copy

    for load in loads[3:]:
        load.wait()
    tables(slot_ref, target_ref, table)
    fill = pltpu.make_async_copy(table, table_s, local_sem.at[6])
    fill.start()

    rows = tiles.reshape(count * BLOCK, 2 * BLOCK)

    @pl.loop(0, count // 16)
    def _(a):
        first = pl.multiple_of(a * 16, 16)
        for i in range(0, BLOCK, 2):
            pair = flat[pl.ds(first, 16), i * BLOCK : (i + 2) * BLOCK].astype(jnp.float32)
            rows[pl.ds(first * BLOCK + i, 16, stride=BLOCK), :] = pair
            rows[pl.ds(first * BLOCK + i + 1, 16, stride=BLOCK), :] = pltpu.roll(pair, BLOCK, 1)

    fill.wait()

    def edge_copies(c, side, piece):
        part = pl.ds(piece * PIECE, PIECE)
        return [
            pltpu.make_async_remote_copy(
                src_ref=src.at[c, side, part],
                dst_ref=dst.at[c, side, part],
                send_sem=edge_send.at[c, side, piece, n],
                recv_sem=edge_recv.at[c, side, piece, n],
                device_id=(after, before)[side],
                device_id_type=MESH,
            )
            for n, (src, dst) in enumerate(((scale_out, scale_in), (edge_out, edge_in)))
        ]

    edges = []
    for c in range(CHUNKS):
        columns = slice(c * width, (c + 1) * width)
        for k in ORDER:
            sends[c][k].wait_recv()

        def run(step, total):
            for u in range(UNROLL):
                place = step * UNROLL + u
                block = received[c, table_s[1, place]]
                tile = tiles[table_s[0, place]][:, :BLOCK].astype(jnp.bfloat16)
                part = jnp.dot(tile, block, preferred_element_type=jnp.float32)
                total = part + total * table_s[2, place].astype(jnp.float32)
                sums[place] = total
            return total

        lax.fori_loop(0, count // UNROLL, run, jnp.zeros((BLOCK, width), jnp.float32))

        edges.append({})
        for piece, side in PIECES:

            @pl.loop(piece * PIECE, (piece + 1) * PIECE)
            def _(i):
                whole = sums[table_s[3, side * EB + i]]
                most = jnp.maximum(jnp.max(jnp.abs(whole), axis=0, keepdims=True), 1e-30)
                coded = jnp.round(whole * (STEPS / most))
                edge_out[c, side, i] = coded.astype(jnp.int32).astype(jnp.int16)
                scale_out[c, side, i] = most * (1.0 / STEPS)

            edges[c][piece, side] = edge_copies(c, side, piece)
            for copy in edges[c][piece, side]:
                copy.start()

        @pl.loop(0, TB)
        def _(i):
            out_ref[i, :, columns] = sums[table_s[3, 2 * EB + i]]

    for c in range(CHUNKS):
        columns = slice(c * width, (c + 1) * width)
        for piece, side in PIECES:
            for copy in edges[c][piece, side]:
                copy.wait_recv()

            @pl.loop(piece * PIECE, (piece + 1) * PIECE)
            def _(i):
                part = edge_in[c, side, i].astype(jnp.int32).astype(jnp.float32) * scale_in[c, side, i]
                spot = i + (0 if side == 0 else TB - EB)
                out_ref[spot, :, columns] = out_ref[spot, :, columns] + part

    for c in range(CHUNKS):
        for k in ORDER:
            sends[c][k].wait_send()
        for copies in edges[c].values():
            for copy in copies:
                copy.wait_send()


def body(groups, size, source, send_ids, send_counts, tile_slot, tile_target, tile_weights):
    count = tile_weights.shape[0]
    cap = send_ids.shape[1] // size
    width = COLS // CHUNKS
    blocks = source.shape[0] // BLOCK
    vmem = pl.BlockSpec(memory_space=pltpu.VMEM)
    hbm = pl.BlockSpec(memory_space=pltpu.HBM)
    dma = pltpu.SemaphoreType.DMA
    operands = (
        send_ids, send_counts, tile_slot, tile_target,
        source.reshape(blocks, BLOCK, COLS), tile_weights,
    )
    out = pl.pallas_call(
        functools.partial(kernel, groups, size),
        out_shape=jax.ShapeDtypeStruct((TB, BLOCK, COLS), jnp.float32),
        in_specs=[hbm] * 6,
        out_specs=vmem,
        scratch_shapes=[
            pltpu.SMEM(send_ids.shape, jnp.int32),
            pltpu.SMEM(send_counts.shape, jnp.int32),
            pltpu.VMEM(tile_slot.shape, jnp.int32),
            pltpu.VMEM(tile_target.shape, jnp.int32),
            pltpu.VMEM((blocks, BLOCK, COLS), jnp.bfloat16),
            pltpu.VMEM((count, BLOCK * BLOCK), jnp.bfloat16),
            pltpu.VMEM((count, BLOCK, 2 * BLOCK), jnp.float32),
            pltpu.VMEM((CHUNKS, size, cap, BLOCK, width), jnp.bfloat16),
            pltpu.VMEM((CHUNKS, size * cap, BLOCK, width), jnp.bfloat16),
            pltpu.VMEM((count, BLOCK, width), jnp.float32),
            pltpu.VMEM((8, count), jnp.int32),
            pltpu.SMEM((8, count), jnp.int32),
            pltpu.VMEM((CHUNKS, 2, EB, BLOCK, width), jnp.int16),
            pltpu.VMEM((CHUNKS, 2, EB, 1, width), jnp.float32),
            pltpu.VMEM((CHUNKS, 2, EB, BLOCK, width), jnp.int16),
            pltpu.VMEM((CHUNKS, 2, EB, 1, width), jnp.float32),
            dma((7,)),
            dma((CHUNKS, size)),
            dma((CHUNKS, size)),
            dma((CHUNKS, 2, EB // PIECE, 2)),
            dma((CHUNKS, 2, EB // PIECE, 2)),
        ],
        compiler_params=pltpu.CompilerParams(
            collective_id=0, has_side_effects=True, vmem_limit_bytes=48 << 20
        ),
    )(*(pltpu.with_memory_space_constraint(x, pltpu.HBM) for x in operands))
    return out.reshape(TB * BLOCK, COLS)


def solution(mesh):
    sizes = (mesh.shape["grp"], mesh.shape["blk"])
    return jax.shard_map(
        functools.partial(body, *sizes),
        mesh=mesh,
        in_specs=(P(("grp", "blk"), None),) * 6,
        out_specs=P(("grp", "blk"), None),
        check_vma=False,
    )
```

```python
import functools

import jax
import jax.numpy as jnp
from jax import lax
from jax.experimental import pallas as pl
from jax.experimental.pallas import tpu as pltpu
from jax.sharding import PartitionSpec as P

COLS = 256
BLOCK = 64
HALF = BLOCK // 2
TB = 32
EB = 16
SEG = TB + 2 * EB
CHUNKS = 2
UNROLL = 32
ORDER = (4, 3, 5, 2, 6, 1, 7)
STEPS = 32766.0
PIECE = 4
PIECES = [(piece, side) for piece in range(EB // PIECE) for side in range(2)]
MESH = pl.DeviceIdType.MESH


def tables(slot_ref, target_ref, table_ref):
    count = slot_ref.shape[1]
    key = (target_ref[...] + EB) % SEG
    across = jnp.broadcast_to(key, (count, count))
    down = across.T
    row = lax.broadcasted_iota(jnp.int32, (count, count), 0)
    col = lax.broadcasted_iota(jnp.int32, (count, count), 1)
    ahead = (down < across) | ((down == across) & (row < col))
    rank = jnp.sum(ahead.astype(jnp.int32), axis=0, keepdims=True)
    packed = lax.broadcasted_iota(jnp.int32, (1, count), 1) + 128 * slot_ref[...] + 2048 * key
    rank_down = jnp.broadcast_to(rank, (count, count)).T
    packed_down = jnp.broadcast_to(packed, (count, count)).T
    ordered = jnp.sum(jnp.where(rank_down == col, packed_down, 0), axis=0, keepdims=True)
    goal = ordered >> 11
    same = (goal == pltpu.roll(goal, 1, 1)) & (lax.broadcasted_iota(jnp.int32, (1, count), 1) > 0)
    table_ref[0:1, :] = ordered & 127
    table_ref[1:2, :] = (ordered >> 7) & 15
    table_ref[2:3, :] = same.astype(jnp.int32)
    upto = jnp.sum((down <= col).astype(jnp.int32), axis=0, keepdims=True)
    table_ref[3:4, :] = jnp.maximum(upto - 1, 0)


def kernel(
    groups, size,
    ids_hbm, counts_hbm, slot_hbm, target_hbm, source_hbm, weights_hbm, out_ref,
    ids_ref, counts_ref, slot_ref, target_ref, source, flat, tiles, outgoing, received, twice, sums, table, table_s,
    edge_out, scale_out, edge_in, scale_in,
    local_sem, send_sem, recv_sem, edge_send, edge_recv,
):
    group, me = lax.axis_index("grp"), lax.axis_index("blk")
    count = slot_hbm.shape[1]
    width = COLS // CHUNKS
    cap = ids_hbm.shape[1] // size
    after = ((group + (me + 1) // size) % groups, (me + 1) % size)
    before = ((group + groups - 1 + (me + size - 1) // size) % groups, (me + size - 1) % size)

    barrier = pltpu.get_barrier_semaphore()
    for k in range(1, size):
        pl.semaphore_signal(barrier, inc=1, device_id=(group, (me + k) % size), device_id_type=MESH)
    pl.semaphore_signal(barrier, inc=1, device_id=after, device_id_type=MESH)
    pl.semaphore_signal(barrier, inc=1, device_id=before, device_id_type=MESH)

    pairs = (
        (ids_hbm, ids_ref), (counts_hbm, counts_ref), (source_hbm, source),
        (slot_hbm, slot_ref), (target_hbm, target_ref), (weights_hbm, flat),
    )
    loads = [pltpu.make_async_copy(src, dst, local_sem.at[n]) for n, (src, dst) in enumerate(pairs)]
    for load in loads:
        load.start()
    for load in loads[:3]:
        load.wait()

    def pack(c):
        columns = slice(c * width, (c + 1) * width)

        @pl.loop(0, size)
        def _(k):
            reader = (me + k) % size
            live = counts_ref[0, reader]
            for j in range(cap):
                block = source[ids_ref[0, reader * cap + j], :, columns]
                kept = jnp.clip(live - j, 0, 1).astype(jnp.float32)
                outgoing[c, k, j] = block * jnp.full(block.shape, kept, jnp.float32).astype(block.dtype)

    def send(c):
        copies = {}
        for k in ORDER:
            copies[k] = pltpu.make_async_remote_copy(
                src_ref=outgoing.at[c, k],
                dst_ref=received.at[c, pl.ds(me * cap, cap)],
                send_sem=send_sem.at[c, k],
                recv_sem=recv_sem.at[c, k],
                device_id=(group, (me + k) % size),
                device_id_type=MESH,
            )
            copies[k].start()
        for j in range(cap):
            received[c, me * cap + j] = outgoing[c, 0, j]
        return copies

    pack(0)
    pl.semaphore_wait(barrier, size + 1)
    sends = [send(0)]
    pack(1)

    for load in loads[3:]:
        load.wait()
    tables(slot_ref, target_ref, table)
    fill = pltpu.make_async_copy(table, table_s, local_sem.at[6])
    fill.start()

    rows = tiles.reshape(count * HALF, 2 * BLOCK)
    left = lax.broadcasted_iota(jnp.int32, (16, 2 * BLOCK), 1) < BLOCK

    @pl.loop(0, count // 16)
    def _(a):
        first = pl.multiple_of(a * 16, 16)
        for i in range(HALF // 2):
            low, high = (
                flat[pl.ds(first, 16), at * BLOCK : (at + 2) * BLOCK].astype(jnp.float32)
                for at in (2 * i, HALF + 2 * i)
            )
            even = jnp.where(left, low, pltpu.roll(high, BLOCK, 1))
            odd = jnp.where(left, pltpu.roll(low, BLOCK, 1), high)
            rows[pl.ds(first * HALF + 2 * i, 16, stride=HALF), :] = even
            rows[pl.ds(first * HALF + 2 * i + 1, 16, stride=HALF), :] = odd

    @pl.loop(0, size * cap)
    def _(slot):
        twice[slot] = jnp.zeros(twice.shape[1:], twice.dtype)

    sends.append(send(1))
    fill.wait()

    def edge_copies(c, side, piece):
        part = pl.ds(piece * PIECE, PIECE)
        return [
            pltpu.make_async_remote_copy(
                src_ref=src.at[c, side, part],
                dst_ref=dst.at[c, side, part],
                send_sem=edge_send.at[c, side, piece, n],
                recv_sem=edge_recv.at[c, side, piece, n],
                device_id=(after, before)[side],
                device_id_type=MESH,
            )
            for n, (src, dst) in enumerate(((scale_out, scale_in), (edge_out, edge_in)))
        ]

    edges = []
    for c in range(CHUNKS):
        for k in ORDER:
            sends[c][k].wait_recv()

        @pl.loop(0, size * cap)
        def _(slot):
            block = received[c, slot]
            twice[slot, :BLOCK, :width] = block
            twice[slot, BLOCK:, width:] = block

        def run(step, total):
            for u in range(UNROLL):
                place = step * UNROLL + u
                tile = tiles[table_s[0, place]].astype(jnp.bfloat16)
                part = jnp.dot(tile, twice[table_s[1, place]], preferred_element_type=jnp.float32)
                total = part + total * table_s[2, place].astype(jnp.float32)
                sums[c, place] = total
            return total

        lax.fori_loop(0, count // UNROLL, run, jnp.zeros((HALF, 2 * width), jnp.float32))

        edges.append({})
        for piece, side in PIECES:

            @pl.loop(piece * PIECE, (piece + 1) * PIECE)
            def _(i):
                whole = sums[c, table_s[3, side * EB + i]]
                most = jnp.maximum(jnp.max(jnp.abs(whole), axis=0, keepdims=True), 1e-30)
                coded = jnp.round(whole * (STEPS / most))
                edge_out[c, side, i] = coded.astype(jnp.int32).astype(jnp.int16)
                scale_out[c, side, i] = most * (1.0 / STEPS)

            edges[c][piece, side] = edge_copies(c, side, piece)
            for copy in edges[c][piece, side]:
                copy.start()

    for c in range(CHUNKS):
        columns = slice(c * width, (c + 1) * width)

        @pl.loop(0, TB)
        def _(i):
            whole = sums[c, table_s[3, 2 * EB + i]]
            for h in range(2):
                out_ref[i, h * HALF : (h + 1) * HALF, columns] = whole[:, h * width : (h + 1) * width]

    for c in range(CHUNKS):
        columns = slice(c * width, (c + 1) * width)
        for piece, side in PIECES:
            for copy in edges[c][piece, side]:
                copy.wait_recv()

            @pl.loop(piece * PIECE, (piece + 1) * PIECE)
            def _(i):
                part = edge_in[c, side, i].astype(jnp.int32).astype(jnp.float32) * scale_in[c, side, i]
                spot = i + (0 if side == 0 else TB - EB)
                for h in range(2):
                    lines = slice(h * HALF, (h + 1) * HALF)
                    extra = part[:, h * width : (h + 1) * width]
                    out_ref[spot, lines, columns] = out_ref[spot, lines, columns] + extra

    for c in range(CHUNKS):
        for k in ORDER:
            sends[c][k].wait_send()
        for copies in edges[c].values():
            for copy in copies:
                copy.wait_send()


def body(groups, size, source, send_ids, send_counts, tile_slot, tile_target, tile_weights):
    count = tile_weights.shape[0]
    cap = send_ids.shape[1] // size
    width = COLS // CHUNKS
    blocks = source.shape[0] // BLOCK
    vmem = pl.BlockSpec(memory_space=pltpu.VMEM)
    hbm = pl.BlockSpec(memory_space=pltpu.HBM)
    dma = pltpu.SemaphoreType.DMA
    operands = (
        send_ids, send_counts, tile_slot, tile_target,
        source.reshape(blocks, BLOCK, COLS), tile_weights,
    )
    out = pl.pallas_call(
        functools.partial(kernel, groups, size),
        out_shape=jax.ShapeDtypeStruct((TB, BLOCK, COLS), jnp.float32),
        in_specs=[hbm] * 6,
        out_specs=vmem,
        scratch_shapes=[
            pltpu.SMEM(send_ids.shape, jnp.int32),
            pltpu.SMEM(send_counts.shape, jnp.int32),
            pltpu.VMEM(tile_slot.shape, jnp.int32),
            pltpu.VMEM(tile_target.shape, jnp.int32),
            pltpu.VMEM((blocks, BLOCK, COLS), jnp.bfloat16),
            pltpu.VMEM((count, BLOCK * BLOCK), jnp.bfloat16),
            pltpu.VMEM((count, HALF, 2 * BLOCK), jnp.float32),
            pltpu.VMEM((CHUNKS, size, cap, BLOCK, width), jnp.bfloat16),
            pltpu.VMEM((CHUNKS, size * cap, BLOCK, width), jnp.bfloat16),
            pltpu.VMEM((size * cap, 2 * BLOCK, 2 * width), jnp.bfloat16),
            pltpu.VMEM((CHUNKS, count, HALF, 2 * width), jnp.float32),
            pltpu.VMEM((8, count), jnp.int32),
            pltpu.SMEM((8, count), jnp.int32),
            pltpu.VMEM((CHUNKS, 2, EB, HALF, 2 * width), jnp.int16),
            pltpu.VMEM((CHUNKS, 2, EB, 1, 2 * width), jnp.float32),
            pltpu.VMEM((CHUNKS, 2, EB, HALF, 2 * width), jnp.int16),
            pltpu.VMEM((CHUNKS, 2, EB, 1, 2 * width), jnp.float32),
            dma((7,)),
            dma((CHUNKS, size)),
            dma((CHUNKS, size)),
            dma((CHUNKS, 2, EB // PIECE, 2)),
            dma((CHUNKS, 2, EB // PIECE, 2)),
        ],
        compiler_params=pltpu.CompilerParams(
            collective_id=0, has_side_effects=True, vmem_limit_bytes=48 << 20
        ),
    )(*(pltpu.with_memory_space_constraint(x, pltpu.HBM) for x in operands))
    return out.reshape(TB * BLOCK, COLS)


def solution(mesh):
    sizes = (mesh.shape["grp"], mesh.shape["blk"])
    return jax.shard_map(
        functools.partial(body, *sizes),
        mesh=mesh,
        in_specs=(P(("grp", "blk"), None),) * 6,
        out_specs=P(("grp", "blk"), None),
        check_vma=False,
    )
```

```python
import functools

import jax
import jax.numpy as jnp
from jax import lax
from jax.experimental import pallas as pl
from jax.experimental.pallas import tpu as pltpu
from jax.sharding import PartitionSpec as P

COLS = 256
BLOCK = 64
HALF = BLOCK // 2
TB = 32
EB = 16
SEG = TB + 2 * EB
CHUNKS = 2
UNROLL = 32
ORDER = (4, 3, 5, 2, 6, 1, 7)
STEPS = 32766.0
PIECE = 4
PIECES = [(piece, side) for piece in range(EB // PIECE) for side in range(2)]
MESH = pl.DeviceIdType.MESH


def tables(slot_ref, target_ref, table_ref):
    count = slot_ref.shape[1]
    key = (target_ref[...] + EB) % SEG
    across = jnp.broadcast_to(key, (count, count))
    down = across.T
    row = lax.broadcasted_iota(jnp.int32, (count, count), 0)
    col = lax.broadcasted_iota(jnp.int32, (count, count), 1)
    ahead = (down < across) | ((down == across) & (row < col))
    rank = jnp.sum(ahead.astype(jnp.int32), axis=0, keepdims=True)
    packed = lax.broadcasted_iota(jnp.int32, (1, count), 1) + 128 * slot_ref[...] + 2048 * key
    rank_down = jnp.broadcast_to(rank, (count, count)).T
    packed_down = jnp.broadcast_to(packed, (count, count)).T
    ordered = jnp.sum(jnp.where(rank_down == col, packed_down, 0), axis=0, keepdims=True)
    goal = ordered >> 11
    same = (goal == pltpu.roll(goal, 1, 1)) & (lax.broadcasted_iota(jnp.int32, (1, count), 1) > 0)
    table_ref[0:1, :] = ordered & 127
    table_ref[1:2, :] = (ordered >> 7) & 15
    table_ref[2:3, :] = same.astype(jnp.int32)
    upto = jnp.sum((down <= col).astype(jnp.int32), axis=0, keepdims=True)
    table_ref[3:4, :] = jnp.maximum(upto - 1, 0)


def kernel(
    groups, size,
    ids_hbm, counts_hbm, slot_hbm, target_hbm, source_hbm, weights_hbm, out_ref,
    ids_ref, counts_ref, slot_ref, target_ref, source, flat, tiles, outgoing, received, twice, sums, table, table_s,
    edge_out, scale_out, edge_in, scale_in,
    local_sem, send_sem, recv_sem, edge_send, edge_recv, ready,
):
    group, me = lax.axis_index("grp"), lax.axis_index("blk")
    count = slot_hbm.shape[1]
    width = COLS // CHUNKS
    cap = ids_hbm.shape[1] // size
    after = ((group + (me + 1) // size) % groups, (me + 1) % size)
    before = ((group + groups - 1 + (me + size - 1) // size) % groups, (me + size - 1) % size)

    barrier = pltpu.get_barrier_semaphore()
    outer = (me == 0) | (me == size - 1)
    for k in range(1, size):
        peer = (me + k) % size

        @pl.when((peer != 0) & (peer != size - 1))
        def _():
            pl.semaphore_signal(barrier, inc=1, device_id=(group, peer), device_id_type=MESH)

    @pl.when(me == 0)
    def _():
        pl.semaphore_signal(barrier, inc=1, device_id=before, device_id_type=MESH)

    @pl.when(me == size - 1)
    def _():
        pl.semaphore_signal(barrier, inc=1, device_id=after, device_id_type=MESH)

    pairs = (
        (ids_hbm, ids_ref), (counts_hbm, counts_ref), (source_hbm, source),
        (slot_hbm, slot_ref), (target_hbm, target_ref), (weights_hbm, flat),
    )
    loads = [pltpu.make_async_copy(src, dst, local_sem.at[n]) for n, (src, dst) in enumerate(pairs)]
    for load in loads:
        load.start()
    for load in loads[:3]:
        load.wait()

    def pack(c):
        columns = slice(c * width, (c + 1) * width)

        @pl.loop(0, size)
        def _(k):
            reader = (me + k) % size
            live = counts_ref[0, reader]
            for j in range(cap):
                block = source[ids_ref[0, reader * cap + j], :, columns]
                kept = jnp.clip(live - j, 0, 1).astype(jnp.float32)
                outgoing[c, k, j] = block * jnp.full(block.shape, kept, jnp.float32).astype(block.dtype)

    def send(c):
        copies = {}
        for k in ORDER:
            copies[k] = pltpu.make_async_remote_copy(
                src_ref=outgoing.at[c, k],
                dst_ref=received.at[c, pl.ds(me * cap, cap)],
                send_sem=send_sem.at[c, k],
                recv_sem=recv_sem.at[c, k],
                device_id=(group, (me + k) % size),
                device_id_type=MESH,
            )
            copies[k].start()
        for j in range(cap):
            received[c, me * cap + j] = outgoing[c, 0, j]
        return copies

    pack(0)

    @pl.when(jnp.logical_not(outer))
    def _():
        pl.semaphore_wait(barrier, size - 1)

    @pl.when(me == 1)
    def _():
        pl.semaphore_signal(ready, inc=1, device_id=(group, 0), device_id_type=MESH)

    @pl.when(me == size - 2)
    def _():
        pl.semaphore_signal(ready, inc=1, device_id=(group, size - 1), device_id_type=MESH)

    @pl.when(outer)
    def _():
        pl.semaphore_wait(ready, 1)

    sends = [send(0)]
    pack(1)

    for load in loads[3:]:
        load.wait()
    tables(slot_ref, target_ref, table)
    fill = pltpu.make_async_copy(table, table_s, local_sem.at[6])
    fill.start()

    rows = tiles.reshape(count * HALF, 2 * BLOCK)
    left = lax.broadcasted_iota(jnp.int32, (16, 2 * BLOCK), 1) < BLOCK

    @pl.loop(0, count // 16)
    def _(a):
        first = pl.multiple_of(a * 16, 16)
        for i in range(HALF // 2):
            low, high = (
                flat[pl.ds(first, 16), at * BLOCK : (at + 2) * BLOCK].astype(jnp.float32)
                for at in (2 * i, HALF + 2 * i)
            )
            even = jnp.where(left, low, pltpu.roll(high, BLOCK, 1))
            odd = jnp.where(left, pltpu.roll(low, BLOCK, 1), high)
            rows[pl.ds(first * HALF + 2 * i, 16, stride=HALF), :] = even
            rows[pl.ds(first * HALF + 2 * i + 1, 16, stride=HALF), :] = odd

    @pl.loop(0, size * cap)
    def _(slot):
        twice[slot] = jnp.zeros(twice.shape[1:], twice.dtype)

    sends.append(send(1))
    fill.wait()

    def edge_copies(c, side, piece):
        part = pl.ds(piece * PIECE, PIECE)
        return [
            pltpu.make_async_remote_copy(
                src_ref=src.at[c, side, part],
                dst_ref=dst.at[c, side, part],
                send_sem=edge_send.at[c, side, piece, n],
                recv_sem=edge_recv.at[c, side, piece, n],
                device_id=(after, before)[side],
                device_id_type=MESH,
            )
            for n, (src, dst) in enumerate(((scale_out, scale_in), (edge_out, edge_in)))
        ]

    edges = []
    for c in range(CHUNKS):
        for k in ORDER:
            sends[c][k].wait_recv()

        @pl.loop(0, size * cap)
        def _(slot):
            block = received[c, slot]
            twice[slot, :BLOCK, :width] = block
            twice[slot, BLOCK:, width:] = block

        def run(step, total):
            for u in range(UNROLL):
                place = step * UNROLL + u
                tile = tiles[table_s[0, place]].astype(jnp.bfloat16)
                part = jnp.dot(tile, twice[table_s[1, place]], preferred_element_type=jnp.float32)
                total = part + total * table_s[2, place].astype(jnp.float32)
                sums[c, place] = total
            return total

        lax.fori_loop(0, count // UNROLL, run, jnp.zeros((HALF, 2 * width), jnp.float32))

        if c == 0:

            @pl.when(outer)
            def _():
                pl.semaphore_wait(barrier, 1)

        edges.append({})
        for piece, side in PIECES:

            @pl.loop(piece * PIECE, (piece + 1) * PIECE)
            def _(i):
                whole = sums[c, table_s[3, side * EB + i]]
                most = jnp.maximum(jnp.max(jnp.abs(whole), axis=0, keepdims=True), 1e-30)
                coded = jnp.round(whole * (STEPS / most))
                edge_out[c, side, i] = coded.astype(jnp.int32).astype(jnp.int16)
                scale_out[c, side, i] = most * (1.0 / STEPS)

            edges[c][piece, side] = edge_copies(c, side, piece)
            for copy in edges[c][piece, side]:
                copy.start()

    for c in range(CHUNKS):
        columns = slice(c * width, (c + 1) * width)

        @pl.loop(0, TB)
        def _(i):
            whole = sums[c, table_s[3, 2 * EB + i]]
            for h in range(2):
                out_ref[i, h * HALF : (h + 1) * HALF, columns] = whole[:, h * width : (h + 1) * width]

    for c in range(CHUNKS):
        columns = slice(c * width, (c + 1) * width)
        for piece, side in PIECES:
            for copy in edges[c][piece, side]:
                copy.wait_recv()

            @pl.loop(piece * PIECE, (piece + 1) * PIECE)
            def _(i):
                part = edge_in[c, side, i].astype(jnp.int32).astype(jnp.float32) * scale_in[c, side, i]
                spot = i + (0 if side == 0 else TB - EB)
                for h in range(2):
                    lines = slice(h * HALF, (h + 1) * HALF)
                    extra = part[:, h * width : (h + 1) * width]
                    out_ref[spot, lines, columns] = out_ref[spot, lines, columns] + extra

    for c in range(CHUNKS):
        for k in ORDER:
            sends[c][k].wait_send()
        for copies in edges[c].values():
            for copy in copies:
                copy.wait_send()


def body(groups, size, source, send_ids, send_counts, tile_slot, tile_target, tile_weights):
    count = tile_weights.shape[0]
    cap = send_ids.shape[1] // size
    width = COLS // CHUNKS
    blocks = source.shape[0] // BLOCK
    vmem = pl.BlockSpec(memory_space=pltpu.VMEM)
    hbm = pl.BlockSpec(memory_space=pltpu.HBM)
    dma = pltpu.SemaphoreType.DMA
    operands = (
        send_ids, send_counts, tile_slot, tile_target,
        source.reshape(blocks, BLOCK, COLS), tile_weights,
    )
    out = pl.pallas_call(
        functools.partial(kernel, groups, size),
        out_shape=jax.ShapeDtypeStruct((TB, BLOCK, COLS), jnp.float32),
        in_specs=[hbm] * 6,
        out_specs=vmem,
        scratch_shapes=[
            pltpu.SMEM(send_ids.shape, jnp.int32),
            pltpu.SMEM(send_counts.shape, jnp.int32),
            pltpu.VMEM(tile_slot.shape, jnp.int32),
            pltpu.VMEM(tile_target.shape, jnp.int32),
            pltpu.VMEM((blocks, BLOCK, COLS), jnp.bfloat16),
            pltpu.VMEM((count, BLOCK * BLOCK), jnp.bfloat16),
            pltpu.VMEM((count, HALF, 2 * BLOCK), jnp.float32),
            pltpu.VMEM((CHUNKS, size, cap, BLOCK, width), jnp.bfloat16),
            pltpu.VMEM((CHUNKS, size * cap, BLOCK, width), jnp.bfloat16),
            pltpu.VMEM((size * cap, 2 * BLOCK, 2 * width), jnp.bfloat16),
            pltpu.VMEM((CHUNKS, count, HALF, 2 * width), jnp.float32),
            pltpu.VMEM((8, count), jnp.int32),
            pltpu.SMEM((8, count), jnp.int32),
            pltpu.VMEM((CHUNKS, 2, EB, HALF, 2 * width), jnp.int16),
            pltpu.VMEM((CHUNKS, 2, EB, 1, 2 * width), jnp.float32),
            pltpu.VMEM((CHUNKS, 2, EB, HALF, 2 * width), jnp.int16),
            pltpu.VMEM((CHUNKS, 2, EB, 1, 2 * width), jnp.float32),
            dma((7,)),
            dma((CHUNKS, size)),
            dma((CHUNKS, size)),
            dma((CHUNKS, 2, EB // PIECE, 2)),
            dma((CHUNKS, 2, EB // PIECE, 2)),
            pltpu.SemaphoreType.REGULAR,
        ],
        compiler_params=pltpu.CompilerParams(
            collective_id=0, has_side_effects=True, vmem_limit_bytes=48 << 20
        ),
    )(*(pltpu.with_memory_space_constraint(x, pltpu.HBM) for x in operands))
    return out.reshape(TB * BLOCK, COLS)


def solution(mesh):
    sizes = (mesh.shape["grp"], mesh.shape["blk"])
    return jax.shard_map(
        functools.partial(body, *sizes),
        mesh=mesh,
        in_specs=(P(("grp", "blk"), None),) * 6,
        out_specs=P(("grp", "blk"), None),
        check_vma=False,
    )
```

```python
import functools

import jax
import jax.numpy as jnp
from jax import lax
from jax.experimental import pallas as pl
from jax.experimental.pallas import tpu as pltpu
from jax.sharding import PartitionSpec as P

COLS = 256
BLOCK = 64
HALF = BLOCK // 2
TB = 32
EB = 16
SEG = TB + 2 * EB
CHUNKS = 2
UNROLL = 32
ORDER = (4, 3, 5, 2, 6, 1, 7)
STEPS = 32766.0
PIECE = 4
PIECES = [(piece, side) for piece in range(EB // PIECE) for side in range(2)]
MESH = pl.DeviceIdType.MESH


def tables(slot_ref, target_ref, table_ref):
    count = slot_ref.shape[1]
    key = (target_ref[...] + EB) % SEG
    across = jnp.broadcast_to(key, (count, count))
    down = across.T
    row = lax.broadcasted_iota(jnp.int32, (count, count), 0)
    col = lax.broadcasted_iota(jnp.int32, (count, count), 1)
    ahead = (down < across) | ((down == across) & (row < col))
    rank = jnp.sum(ahead.astype(jnp.int32), axis=0, keepdims=True)
    packed = lax.broadcasted_iota(jnp.int32, (1, count), 1) + 128 * slot_ref[...] + 2048 * key
    rank_down = jnp.broadcast_to(rank, (count, count)).T
    packed_down = jnp.broadcast_to(packed, (count, count)).T
    ordered = jnp.sum(jnp.where(rank_down == col, packed_down, 0), axis=0, keepdims=True)
    goal = ordered >> 11
    same = (goal == pltpu.roll(goal, 1, 1)) & (lax.broadcasted_iota(jnp.int32, (1, count), 1) > 0)
    table_ref[0:1, :] = ordered & 127
    table_ref[1:2, :] = (ordered >> 7) & 15
    table_ref[2:3, :] = same.astype(jnp.int32)
    upto = jnp.sum((down <= col).astype(jnp.int32), axis=0, keepdims=True)
    table_ref[3:4, :] = jnp.maximum(upto - 1, 0)


def kernel(
    groups, size,
    ids_hbm, counts_hbm, slot_hbm, target_hbm, source_hbm, weights_hbm, out_ref,
    ids_ref, counts_ref, slot_ref, target_ref, source, flat, tiles, outgoing, received, twice, sums, table, table_s,
    edge_out, scale_out, edge_in, scale_in,
    local_sem, send_sem, recv_sem, edge_send, edge_recv, ready,
):
    group, me = lax.axis_index("grp"), lax.axis_index("blk")
    count = slot_hbm.shape[1]
    width = COLS // CHUNKS
    cap = ids_hbm.shape[1] // size
    after = ((group + (me + 1) // size) % groups, (me + 1) % size)
    before = ((group + groups - 1 + (me + size - 1) // size) % groups, (me + size - 1) % size)

    barrier = pltpu.get_barrier_semaphore()
    outer = (me == 0) | (me == size - 1)
    for k in range(1, size):
        peer = (me + k) % size

        @pl.when((peer != 0) & (peer != size - 1))
        def _():
            pl.semaphore_signal(barrier, inc=1, device_id=(group, peer), device_id_type=MESH)

    pairs = (
        (ids_hbm, ids_ref), (counts_hbm, counts_ref), (source_hbm, source),
        (slot_hbm, slot_ref), (target_hbm, target_ref), (weights_hbm, flat),
    )
    loads = [pltpu.make_async_copy(src, dst, local_sem.at[n]) for n, (src, dst) in enumerate(pairs)]
    for load in loads:
        load.start()
    for load in loads[:3]:
        load.wait()

    def pack(c):
        columns = slice(c * width, (c + 1) * width)

        @pl.loop(0, size)
        def _(k):
            reader = (me + k) % size
            live = counts_ref[0, reader]
            for j in range(cap):
                block = source[ids_ref[0, reader * cap + j], :, columns]
                kept = jnp.clip(live - j, 0, 1).astype(jnp.float32)
                outgoing[c, k, j] = block * jnp.full(block.shape, kept, jnp.float32).astype(block.dtype)

    def send(c):
        copies = {}
        for k in ORDER:
            copies[k] = pltpu.make_async_remote_copy(
                src_ref=outgoing.at[c, k],
                dst_ref=received.at[c, pl.ds(me * cap, cap)],
                send_sem=send_sem.at[c, k],
                recv_sem=recv_sem.at[c, k],
                device_id=(group, (me + k) % size),
                device_id_type=MESH,
            )
            copies[k].start()
        for j in range(cap):
            received[c, me * cap + j] = outgoing[c, 0, j]
        return copies

    pack(0)

    @pl.when(jnp.logical_not(outer))
    def _():
        pl.semaphore_wait(barrier, size - 1)

    @pl.when(me == 1)
    def _():
        pl.semaphore_signal(ready, inc=1, device_id=(group, 0), device_id_type=MESH)

    @pl.when(me == size - 2)
    def _():
        pl.semaphore_signal(ready, inc=1, device_id=(group, size - 1), device_id_type=MESH)

    @pl.when(outer)
    def _():
        pl.semaphore_wait(ready, 1)

    sends = [send(0)]
    pack(1)

    for load in loads[3:]:
        load.wait()
    tables(slot_ref, target_ref, table)
    fill = pltpu.make_async_copy(table, table_s, local_sem.at[6])
    fill.start()

    rows = tiles.reshape(count * HALF, 2 * BLOCK)
    left = lax.broadcasted_iota(jnp.int32, (16, 2 * BLOCK), 1) < BLOCK

    @pl.loop(0, count // 16)
    def _(a):
        first = pl.multiple_of(a * 16, 16)
        for i in range(HALF // 2):
            low, high = (
                flat[pl.ds(first, 16), at * BLOCK : (at + 2) * BLOCK].astype(jnp.float32)
                for at in (2 * i, HALF + 2 * i)
            )
            even = jnp.where(left, low, pltpu.roll(high, BLOCK, 1))
            odd = jnp.where(left, pltpu.roll(low, BLOCK, 1), high)
            rows[pl.ds(first * HALF + 2 * i, 16, stride=HALF), :] = even
            rows[pl.ds(first * HALF + 2 * i + 1, 16, stride=HALF), :] = odd

    @pl.loop(0, size * cap)
    def _(slot):
        twice[slot] = jnp.zeros(twice.shape[1:], twice.dtype)

    sends.append(send(1))
    fill.wait()

    def edge_copies(c, side, piece):
        part = pl.ds(piece * PIECE, PIECE)
        return [
            pltpu.make_async_remote_copy(
                src_ref=src.at[c, side, part],
                dst_ref=dst.at[c, side, part],
                send_sem=edge_send.at[c, side, piece, n],
                recv_sem=edge_recv.at[c, side, piece, n],
                device_id=(after, before)[side],
                device_id_type=MESH,
            )
            for n, (src, dst) in enumerate(((scale_out, scale_in), (edge_out, edge_in)))
        ]

    edges = []
    for c in range(CHUNKS):
        for k in ORDER:
            sends[c][k].wait_recv()

        if c == 0:

            @pl.when(me == 0)
            def _():
                pl.semaphore_signal(barrier, inc=1, device_id=before, device_id_type=MESH)

            @pl.when(me == size - 1)
            def _():
                pl.semaphore_signal(barrier, inc=1, device_id=after, device_id_type=MESH)

        @pl.loop(0, size * cap)
        def _(slot):
            block = received[c, slot]
            twice[slot, :BLOCK, :width] = block
            twice[slot, BLOCK:, width:] = block

        def run(step, total):
            for u in range(UNROLL):
                place = step * UNROLL + u
                tile = tiles[table_s[0, place]].astype(jnp.bfloat16)
                part = jnp.dot(tile, twice[table_s[1, place]], preferred_element_type=jnp.float32)
                total = part + total * table_s[2, place].astype(jnp.float32)
                sums[c, place] = total
            return total

        lax.fori_loop(0, count // UNROLL, run, jnp.zeros((HALF, 2 * width), jnp.float32))

        if c == 0:

            @pl.when(me == size - 1)
            def _():
                pl.semaphore_wait(barrier, 1)

        edges.append({})
        for piece, side in PIECES:

            @pl.loop(piece * PIECE, (piece + 1) * PIECE)
            def _(i):
                whole = sums[c, table_s[3, side * EB + i]]
                most = jnp.maximum(jnp.max(jnp.abs(whole), axis=0, keepdims=True), 1e-30)
                coded = jnp.round(whole * (STEPS / most))
                edge_out[c, side, i] = coded.astype(jnp.int32).astype(jnp.int16)
                scale_out[c, side, i] = most * (1.0 / STEPS)

            edges[c][piece, side] = edge_copies(c, side, piece)

            @pl.when((side == 0) | (me != 0))
            def _():
                for copy in edges[c][piece, side]:
                    copy.start()

    @pl.when(me == 0)
    def _():
        pl.semaphore_wait(barrier, 1)
        for c in range(CHUNKS):
            for piece in range(EB // PIECE):
                for copy in edges[c][piece, 1]:
                    copy.start()

    for c in range(CHUNKS):
        columns = slice(c * width, (c + 1) * width)

        @pl.loop(0, TB)
        def _(i):
            whole = sums[c, table_s[3, 2 * EB + i]]
            for h in range(2):
                out_ref[i, h * HALF : (h + 1) * HALF, columns] = whole[:, h * width : (h + 1) * width]

    for c in range(CHUNKS):
        columns = slice(c * width, (c + 1) * width)
        for piece, side in PIECES:
            for copy in edges[c][piece, side]:
                copy.wait_recv()

            @pl.loop(piece * PIECE, (piece + 1) * PIECE)
            def _(i):
                part = edge_in[c, side, i].astype(jnp.int32).astype(jnp.float32) * scale_in[c, side, i]
                spot = i + (0 if side == 0 else TB - EB)
                for h in range(2):
                    lines = slice(h * HALF, (h + 1) * HALF)
                    extra = part[:, h * width : (h + 1) * width]
                    out_ref[spot, lines, columns] = out_ref[spot, lines, columns] + extra

    for c in range(CHUNKS):
        for k in ORDER:
            sends[c][k].wait_send()
        for copies in edges[c].values():
            for copy in copies:
                copy.wait_send()


def body(groups, size, source, send_ids, send_counts, tile_slot, tile_target, tile_weights):
    count = tile_weights.shape[0]
    cap = send_ids.shape[1] // size
    width = COLS // CHUNKS
    blocks = source.shape[0] // BLOCK
    vmem = pl.BlockSpec(memory_space=pltpu.VMEM)
    hbm = pl.BlockSpec(memory_space=pltpu.HBM)
    dma = pltpu.SemaphoreType.DMA
    operands = (
        send_ids, send_counts, tile_slot, tile_target,
        source.reshape(blocks, BLOCK, COLS), tile_weights,
    )
    out = pl.pallas_call(
        functools.partial(kernel, groups, size),
        out_shape=jax.ShapeDtypeStruct((TB, BLOCK, COLS), jnp.float32),
        in_specs=[hbm] * 6,
        out_specs=vmem,
        scratch_shapes=[
            pltpu.SMEM(send_ids.shape, jnp.int32),
            pltpu.SMEM(send_counts.shape, jnp.int32),
            pltpu.VMEM(tile_slot.shape, jnp.int32),
            pltpu.VMEM(tile_target.shape, jnp.int32),
            pltpu.VMEM((blocks, BLOCK, COLS), jnp.bfloat16),
            pltpu.VMEM((count, BLOCK * BLOCK), jnp.bfloat16),
            pltpu.VMEM((count, HALF, 2 * BLOCK), jnp.float32),
            pltpu.VMEM((CHUNKS, size, cap, BLOCK, width), jnp.bfloat16),
            pltpu.VMEM((CHUNKS, size * cap, BLOCK, width), jnp.bfloat16),
            pltpu.VMEM((size * cap, 2 * BLOCK, 2 * width), jnp.bfloat16),
            pltpu.VMEM((CHUNKS, count, HALF, 2 * width), jnp.float32),
            pltpu.VMEM((8, count), jnp.int32),
            pltpu.SMEM((8, count), jnp.int32),
            pltpu.VMEM((CHUNKS, 2, EB, HALF, 2 * width), jnp.int16),
            pltpu.VMEM((CHUNKS, 2, EB, 1, 2 * width), jnp.float32),
            pltpu.VMEM((CHUNKS, 2, EB, HALF, 2 * width), jnp.int16),
            pltpu.VMEM((CHUNKS, 2, EB, 1, 2 * width), jnp.float32),
            dma((7,)),
            dma((CHUNKS, size)),
            dma((CHUNKS, size)),
            dma((CHUNKS, 2, EB // PIECE, 2)),
            dma((CHUNKS, 2, EB // PIECE, 2)),
            pltpu.SemaphoreType.REGULAR,
        ],
        compiler_params=pltpu.CompilerParams(
            collective_id=0, has_side_effects=True, vmem_limit_bytes=48 << 20
        ),
    )(*(pltpu.with_memory_space_constraint(x, pltpu.HBM) for x in operands))
    return out.reshape(TB * BLOCK, COLS)


def solution(mesh):
    sizes = (mesh.shape["grp"], mesh.shape["blk"])
    return jax.shard_map(
        functools.partial(body, *sizes),
        mesh=mesh,
        in_specs=(P(("grp", "blk"), None),) * 6,
        out_specs=P(("grp", "blk"), None),
        check_vma=False,
    )
```

```python
import functools

import jax
import jax.numpy as jnp
from jax import lax
from jax.experimental import pallas as pl
from jax.experimental.pallas import tpu as pltpu
from jax.sharding import PartitionSpec as P

COLS = 256
BLOCK = 64
HALF = BLOCK // 2
TB = 32
EB = 16
SEG = TB + 2 * EB
CHUNKS = 2
UNROLL = 64
ORDER = (4, 3, 5, 2, 6, 1, 7)
STEPS = 32766.0
PIECE = 4
PIECES = [(piece, side) for piece in range(EB // PIECE) for side in range(2)]
MESH = pl.DeviceIdType.MESH


def tables(slot_ref, target_ref, table_ref):
    count = slot_ref.shape[1]
    key = (target_ref[...] + EB) % SEG
    across = jnp.broadcast_to(key, (count, count))
    down = across.T
    row = lax.broadcasted_iota(jnp.int32, (count, count), 0)
    col = lax.broadcasted_iota(jnp.int32, (count, count), 1)
    ahead = (down < across) | ((down == across) & (row < col))
    rank = jnp.sum(ahead.astype(jnp.int32), axis=0, keepdims=True)
    packed = lax.broadcasted_iota(jnp.int32, (1, count), 1) + 128 * slot_ref[...] + 2048 * key
    rank_down = jnp.broadcast_to(rank, (count, count)).T
    packed_down = jnp.broadcast_to(packed, (count, count)).T
    ordered = jnp.sum(jnp.where(rank_down == col, packed_down, 0), axis=0, keepdims=True)
    goal = ordered >> 11
    same = (goal == pltpu.roll(goal, 1, 1)) & (lax.broadcasted_iota(jnp.int32, (1, count), 1) > 0)
    table_ref[0:1, :] = ordered & 127
    table_ref[1:2, :] = (ordered >> 7) & 15
    table_ref[2:3, :] = same.astype(jnp.int32)
    upto = jnp.sum((down <= col).astype(jnp.int32), axis=0, keepdims=True)
    table_ref[3:4, :] = jnp.maximum(upto - 1, 0)


def kernel(
    groups, size,
    ids_hbm, counts_hbm, slot_hbm, target_hbm, source_hbm, weights_hbm, out_ref,
    ids_ref, counts_ref, slot_ref, target_ref, source, flat, tiles, outgoing, received, twice, sums, table, table_s,
    edge_out, scale_out, edge_in, scale_in,
    local_sem, send_sem, recv_sem, edge_send, edge_recv, ready,
):
    group, me = lax.axis_index("grp"), lax.axis_index("blk")
    count = slot_hbm.shape[1]
    width = COLS // CHUNKS
    cap = ids_hbm.shape[1] // size
    after = ((group + (me + 1) // size) % groups, (me + 1) % size)
    before = ((group + groups - 1 + (me + size - 1) // size) % groups, (me + size - 1) % size)

    barrier = pltpu.get_barrier_semaphore()
    outer = (me == 0) | (me == size - 1)
    for k in range(1, size):
        peer = (me + k) % size

        @pl.when((peer != 0) & (peer != size - 1))
        def _():
            pl.semaphore_signal(barrier, inc=1, device_id=(group, peer), device_id_type=MESH)

    pairs = (
        (ids_hbm, ids_ref), (counts_hbm, counts_ref), (source_hbm, source),
        (slot_hbm, slot_ref), (target_hbm, target_ref), (weights_hbm, flat),
    )
    loads = [pltpu.make_async_copy(src, dst, local_sem.at[n]) for n, (src, dst) in enumerate(pairs)]
    for load in loads:
        load.start()
    for load in loads[:3]:
        load.wait()

    def pack(c):
        columns = slice(c * width, (c + 1) * width)

        @pl.loop(0, size)
        def _(k):
            reader = (me + k) % size
            live = counts_ref[0, reader]
            for j in range(cap):
                block = source[ids_ref[0, reader * cap + j], :, columns]
                kept = jnp.clip(live - j, 0, 1).astype(jnp.float32)
                outgoing[c, k, j] = block * jnp.full(block.shape, kept, jnp.float32).astype(block.dtype)

    def send(c):
        copies = {}
        for k in ORDER:
            copies[k] = pltpu.make_async_remote_copy(
                src_ref=outgoing.at[c, k],
                dst_ref=received.at[c, pl.ds(me * cap, cap)],
                send_sem=send_sem.at[c, k],
                recv_sem=recv_sem.at[c, k],
                device_id=(group, (me + k) % size),
                device_id_type=MESH,
            )
            copies[k].start()
        for j in range(cap):
            received[c, me * cap + j] = outgoing[c, 0, j]
        return copies

    pack(0)

    @pl.when(jnp.logical_not(outer))
    def _():
        pl.semaphore_wait(barrier, size - 1)

    @pl.when(me == 1)
    def _():
        pl.semaphore_signal(ready, inc=1, device_id=(group, 0), device_id_type=MESH)

    @pl.when(me == size - 2)
    def _():
        pl.semaphore_signal(ready, inc=1, device_id=(group, size - 1), device_id_type=MESH)

    @pl.when(outer)
    def _():
        pl.semaphore_wait(ready, 1)

    sends = [send(0)]
    pack(1)

    for load in loads[3:]:
        load.wait()
    tables(slot_ref, target_ref, table)
    fill = pltpu.make_async_copy(table, table_s, local_sem.at[6])
    fill.start()

    rows = tiles.reshape(count * HALF, 2 * BLOCK)
    left = lax.broadcasted_iota(jnp.int32, (16, 2 * BLOCK), 1) < BLOCK

    @pl.loop(0, count // 16)
    def _(a):
        first = pl.multiple_of(a * 16, 16)
        for i in range(HALF // 2):
            low, high = (
                flat[pl.ds(first, 16), at * BLOCK : (at + 2) * BLOCK].astype(jnp.float32)
                for at in (2 * i, HALF + 2 * i)
            )
            even = jnp.where(left, low, pltpu.roll(high, BLOCK, 1))
            odd = jnp.where(left, pltpu.roll(low, BLOCK, 1), high)
            rows[pl.ds(first * HALF + 2 * i, 16, stride=HALF), :] = even
            rows[pl.ds(first * HALF + 2 * i + 1, 16, stride=HALF), :] = odd

    @pl.loop(0, size * cap)
    def _(slot):
        twice[slot] = jnp.zeros(twice.shape[1:], twice.dtype)

    sends.append(send(1))
    fill.wait()

    def edge_copies(c, side, piece):
        part = pl.ds(piece * PIECE, PIECE)
        return [
            pltpu.make_async_remote_copy(
                src_ref=src.at[c, side, part],
                dst_ref=dst.at[c, side, part],
                send_sem=edge_send.at[c, side, piece, n],
                recv_sem=edge_recv.at[c, side, piece, n],
                device_id=(after, before)[side],
                device_id_type=MESH,
            )
            for n, (src, dst) in enumerate(((scale_out, scale_in), (edge_out, edge_in)))
        ]

    edges = []
    for c in range(CHUNKS):
        for k in ORDER:
            sends[c][k].wait_recv()

        if c == 0:

            @pl.when(me == 0)
            def _():
                pl.semaphore_signal(barrier, inc=1, device_id=before, device_id_type=MESH)

            @pl.when(me == size - 1)
            def _():
                pl.semaphore_signal(barrier, inc=1, device_id=after, device_id_type=MESH)

        @pl.loop(0, size * cap, unroll=4)
        def _(slot):
            block = received[c, slot]
            twice[slot, :BLOCK, :width] = block
            twice[slot, BLOCK:, width:] = block

        def run(step, total):
            for u in range(UNROLL):
                place = step * UNROLL + u
                tile = tiles[table_s[0, place]].astype(jnp.bfloat16)
                part = jnp.dot(tile, twice[table_s[1, place]], preferred_element_type=jnp.float32)
                total = part + total * table_s[2, place].astype(jnp.float32)
                sums[c, place] = total
            return total

        lax.fori_loop(0, count // UNROLL, run, jnp.zeros((HALF, 2 * width), jnp.float32))

        if c == 0:

            @pl.when(me == size - 1)
            def _():
                pl.semaphore_wait(barrier, 1)

        edges.append({})
        for piece, side in PIECES:

            @pl.loop(piece * PIECE, (piece + 1) * PIECE, unroll=True)
            def _(i):
                whole = sums[c, table_s[3, side * EB + i]]
                most = jnp.maximum(jnp.max(jnp.abs(whole), axis=0, keepdims=True), 1e-30)
                coded = jnp.round(whole * (STEPS / most))
                edge_out[c, side, i] = coded.astype(jnp.int32).astype(jnp.int16)
                scale_out[c, side, i] = most * (1.0 / STEPS)

            edges[c][piece, side] = edge_copies(c, side, piece)

            @pl.when((side == 0) | (me != 0))
            def _():
                for copy in edges[c][piece, side]:
                    copy.start()

    @pl.when(me == 0)
    def _():
        pl.semaphore_wait(barrier, 1)
        for c in range(CHUNKS):
            for piece in range(EB // PIECE):
                for copy in edges[c][piece, 1]:
                    copy.start()

    for c in range(CHUNKS):
        columns = slice(c * width, (c + 1) * width)

        @pl.loop(0, TB)
        def _(i):
            whole = sums[c, table_s[3, 2 * EB + i]]
            for h in range(2):
                out_ref[i, h * HALF : (h + 1) * HALF, columns] = whole[:, h * width : (h + 1) * width]

    for c in range(CHUNKS):
        columns = slice(c * width, (c + 1) * width)
        for piece, side in PIECES:
            for copy in edges[c][piece, side]:
                copy.wait_recv()

            @pl.loop(piece * PIECE, (piece + 1) * PIECE, unroll=True)
            def _(i):
                part = edge_in[c, side, i].astype(jnp.int32).astype(jnp.float32) * scale_in[c, side, i]
                spot = i + (0 if side == 0 else TB - EB)
                for h in range(2):
                    lines = slice(h * HALF, (h + 1) * HALF)
                    extra = part[:, h * width : (h + 1) * width]
                    out_ref[spot, lines, columns] = out_ref[spot, lines, columns] + extra

    for c in range(CHUNKS):
        for k in ORDER:
            sends[c][k].wait_send()
        for copies in edges[c].values():
            for copy in copies:
                copy.wait_send()


def body(groups, size, source, send_ids, send_counts, tile_slot, tile_target, tile_weights):
    count = tile_weights.shape[0]
    cap = send_ids.shape[1] // size
    width = COLS // CHUNKS
    blocks = source.shape[0] // BLOCK
    vmem = pl.BlockSpec(memory_space=pltpu.VMEM)
    hbm = pl.BlockSpec(memory_space=pltpu.HBM)
    dma = pltpu.SemaphoreType.DMA
    operands = (
        send_ids, send_counts, tile_slot, tile_target,
        source.reshape(blocks, BLOCK, COLS), tile_weights,
    )
    out = pl.pallas_call(
        functools.partial(kernel, groups, size),
        out_shape=jax.ShapeDtypeStruct((TB, BLOCK, COLS), jnp.float32),
        in_specs=[hbm] * 6,
        out_specs=vmem,
        scratch_shapes=[
            pltpu.SMEM(send_ids.shape, jnp.int32),
            pltpu.SMEM(send_counts.shape, jnp.int32),
            pltpu.VMEM(tile_slot.shape, jnp.int32),
            pltpu.VMEM(tile_target.shape, jnp.int32),
            pltpu.VMEM((blocks, BLOCK, COLS), jnp.bfloat16),
            pltpu.VMEM((count, BLOCK * BLOCK), jnp.bfloat16),
            pltpu.VMEM((count, HALF, 2 * BLOCK), jnp.float32),
            pltpu.VMEM((CHUNKS, size, cap, BLOCK, width), jnp.bfloat16),
            pltpu.VMEM((CHUNKS, size * cap, BLOCK, width), jnp.bfloat16),
            pltpu.VMEM((size * cap, 2 * BLOCK, 2 * width), jnp.bfloat16),
            pltpu.VMEM((CHUNKS, count, HALF, 2 * width), jnp.float32),
            pltpu.VMEM((8, count), jnp.int32),
            pltpu.SMEM((8, count), jnp.int32),
            pltpu.VMEM((CHUNKS, 2, EB, HALF, 2 * width), jnp.int16),
            pltpu.VMEM((CHUNKS, 2, EB, 1, 2 * width), jnp.float32),
            pltpu.VMEM((CHUNKS, 2, EB, HALF, 2 * width), jnp.int16),
            pltpu.VMEM((CHUNKS, 2, EB, 1, 2 * width), jnp.float32),
            dma((7,)),
            dma((CHUNKS, size)),
            dma((CHUNKS, size)),
            dma((CHUNKS, 2, EB // PIECE, 2)),
            dma((CHUNKS, 2, EB // PIECE, 2)),
            pltpu.SemaphoreType.REGULAR,
        ],
        compiler_params=pltpu.CompilerParams(
            collective_id=0, has_side_effects=True, vmem_limit_bytes=48 << 20
        ),
    )(*(pltpu.with_memory_space_constraint(x, pltpu.HBM) for x in operands))
    return out.reshape(TB * BLOCK, COLS)


def solution(mesh):
    sizes = (mesh.shape["grp"], mesh.shape["blk"])
    return jax.shard_map(
        functools.partial(body, *sizes),
        mesh=mesh,
        in_specs=(P(("grp", "blk"), None),) * 6,
        out_specs=P(("grp", "blk"), None),
        check_vma=False,
    )
```
